32 devices in a mesh: prow: 4 (over y, core), pcol: 8 (over z, x).
Axes of the slice: x: 2, y: 2, z: 4, core: 2. Of those that a mesh axis runs over, the one named last changes fastest.
Arguments:
- inverse_tiles: float32 [8, 4096, 512], P('prow', 'pcol'), may hold values from -0.36 to 0.36
- tile_rows: int32 [8, 8], P('prow', 'pcol'), may hold values from -1 to 1, as said below
- panel: float32 [4096, 1024], P(('prow', 'pcol')), may hold values from -0.6 to 0.6
- pivot_base: float32 [1024, 512], P('pcol'), may hold values from -6 to 6
Outputs:
- panel_inverse: float32 [4096, 1024], P(('prow', 'pcol'))
- pivot_inverse: float32 [1024, 512], P('pcol')
The draws below stay inside these ranges and needn't reach their ends.
Inputs may be any that keep to these rules, and one draw needn't show every extreme that they name: `tile_rows`: on each device the entries name distinct row tiles first and -1 after; the device at prow 0 and pcol 0 lists 2.
All inputs are finite; a program needn't handle non-finite values.
Results may differ from the reference program's by a relative error of at most 0.0003.
Values sent between devices are 32-bit elements; how exact they have to be, the bound alone decides.
A program may use at most 64 MiB of HBM per device.

```python
import jax
import jax.numpy as jnp
from jax import lax

BS = 512
SUPER = 2
SLOTS = 2
RTILES = 2
ROWS = 4096
N_PROW = 4
N_PCOL = 8


def draw_tile_rows(key, part):
    base = jax.random.fold_in(key, 11)
    key_count, key_first = jax.random.split(base, 2)
    counts = jax.random.randint(key_count, (N_PROW, N_PCOL), 0, 3)
    counts = counts.at[0, 0].set(2)
    first = jax.random.randint(key_first, (N_PROW, N_PCOL), 0, 2)
    slot_zero = jnp.where(counts >= 1, first, -1)
    slot_one = jnp.where(counts == 2, 1 - first, -1)
    return jnp.stack([slot_zero, slot_one], axis=1).reshape(N_PROW * 2, N_PCOL).astype(jnp.int32)


def block_scale(key, dims, cuts, low, top_value):
    factor_of = 1.0
    for position, blocks in cuts:
        steps = jax.random.uniform(jax.random.fold_in(jax.random.fold_in(key, 6), position), (blocks,), jnp.float32, low / len(cuts), top_value / len(cuts))
        factor_of = factor_of * jnp.repeat(jnp.exp(steps), dims[position] // blocks).reshape((-1,) + (1,) * (len(dims) - 1 - position))
    return factor_of


def bell_draw(key, extent, scale, reach, shards=(), kind=jnp.bfloat16):
    result = jax.random.normal(key, extent, jnp.float32) * scale
    if len(shards) > 0:
        result = block_scale(key, extent, shards, -0.22, 0.18) * result
    return jnp.clip(result, min=-reach, max=reach).astype(kind)


def setup_inputs(seed: int = 0) -> dict:
    key_list = jax.random.split(jax.random.key(seed), 5)
    inverse_tiles = bell_draw(key_list[0], (SLOTS * N_PROW, BS * N_PCOL, BS), 0.06, 0.36, ((0, 4), (1, 8)), jnp.float32)
    tile_rows = draw_tile_rows(jax.random.fold_in(key_list[4], 71), 0)
    panel = bell_draw(key_list[2], (ROWS, SUPER * BS), 0.1, 0.6, ((0, 32),), jnp.float32)
    pivot_base = bell_draw(key_list[3], (SUPER * BS, BS), 1.0, 6.0, ((0, 8),), jnp.float32)
    return dict(inverse_tiles=inverse_tiles, tile_rows=tile_rows, panel=panel, pivot_base=pivot_base)


def reference(inverse_tiles, tile_rows, panel, pivot_base):
    grid_rows = N_PROW
    grid_cols = N_PCOL
    width = panel.shape[1]
    share = (2 * BS) // grid_cols
    columns = panel.reshape(grid_rows, grid_cols, share, width).transpose(1, 0, 2, 3).reshape(grid_cols, grid_rows * share, width)
    tiles = inverse_tiles.reshape(grid_rows, SLOTS, grid_cols, BS, BS)
    codes = tile_rows.reshape(grid_rows, SLOTS, grid_cols)
    levels = jnp.arange(RTILES, dtype=jnp.int32)

    def block_row(inputs):
        row_tiles, row_codes = inputs
        products = jnp.einsum("sqab,qbw->sqaw", row_tiles, columns, precision=lax.Precision.HIGHEST)
        placing = (row_codes[:, :, None] == levels[None, None, :]).astype(jnp.float32)
        return jnp.einsum("sqr,sqaw->raw", placing, products, precision=lax.Precision.HIGHEST)

    trailing_product = lax.map(block_row, (tiles, codes)).reshape(panel.shape[0], width)
    panel_inverse = -trailing_product
    upper = panel.reshape(-1, SUPER, BS)
    lower = trailing_product.reshape(-1, SUPER, BS)
    update = jnp.einsum("rka,rkb->kab", upper, lower, precision=lax.Precision.HIGHEST)
    pivot_inverse = pivot_base + update.reshape(SUPER * BS, BS)
    return panel_inverse, pivot_inverse
```

```python
import functools

import jax
import jax.numpy as jnp
from jax import lax
from jax.experimental import pallas as pl
from jax.experimental.pallas import tpu as pltpu
from jax.sharding import PartitionSpec as P

F32 = jnp.float32
BF16 = jnp.bfloat16
PAIR = 2


def split(value):
    high = value.astype(BF16)
    return high, (value - high.astype(F32)).astype(BF16)


def dot3(a_hi, a_lo, b_hi, b_lo):
    dot = functools.partial(jnp.dot, preferred_element_type=F32)
    return dot(a_hi, b_hi) + (dot(a_hi, b_lo) + dot(a_lo, b_hi))


def kernel(rows, cols, tiles, codes, panel, base, out_panel, out_pivot,
           col, srecv, crecv, u, ut_hi, ut_lo, a_hi, a_lo, b_hi, b_lo, part, uprecv, dnrecv,
           piv, prec, xrec, yrec, zrec, fin,
           sem_col, sem_sib, sem_x, sem_y, sem_s, sem_u, sem_us, sem_rs, sem_rss,
           sem_p, sem_px, sem_py, sem_pys, sem_pz, sem_pzs, sem_f, sem_fs, sem_l):
    ny, nz = rows // PAIR, cols // PAIR
    slots, groups, _, share, block = tiles.shape
    width = panel.shape[1]
    chunk = block // PAIR
    supers = width // block
    per_tile = groups * PAIR
    zset = nz // ny
    zj = nz // supers
    pr, pc = lax.axis_index("prow"), lax.axis_index("pcol")
    c, y = lax.rem(pr, PAIR), lax.div(pr, PAIR)
    x, z = lax.rem(pc, PAIR), lax.div(pc, PAIR)
    oc, ox = 1 - c, 1 - x

    def dev(yy=None, cc=None, zz=None, xx=None):
        yy = y if yy is None else yy
        cc = c if cc is None else cc
        zz = z if zz is None else zz
        xx = x if xx is None else xx
        return (yy * PAIR + cc, zz * PAIR + xx)

    sib, xp = dev(cc=oc), dev(xx=ox)
    pending = []

    def remote(src, dst, send, recv, device):
        return pltpu.make_async_remote_copy(
            src_ref=src, dst_ref=dst, send_sem=send, recv_sem=recv,
            device_id=device, device_id_type=pl.DeviceIdType.MESH)

    def send(cond, *args):
        pending.append((cond, args))
        if cond is None:
            remote(*args).start()
        else:
            @pl.when(cond)
            def _():
                remote(*args).start()

    def arrive(dst, recv):
        remote(dst, dst, recv, recv, xp).wait_recv()

    other_y = [lax.rem(y + k, ny) for k in range(1, ny)]
    other_z = [lax.rem(z + k, nz) for k in range(1, nz)]

    barrier = pltpu.get_barrier_semaphore()
    peers = [dev(cc=oc), xp]
    for yy in other_y:
        peers += [dev(yy=yy), dev(yy=yy, cc=oc)]
    peers += [dev(zz=zz) for zz in other_z]
    for peer in peers:
        pl.semaphore_signal(barrier, inc=1, device_id=peer, device_id_type=pl.DeviceIdType.MESH)
    pl.semaphore_wait(barrier, len(peers))

    own = col.at[x, pr]
    send(None, panel, own, sem_x.at[0], sem_col.at[x, pr], xp)
    for k, yy in enumerate(other_y):
        send(None, panel, own, sem_y.at[0, k], sem_col.at[x, pr], dev(yy=yy))
    send(z + 1 < nz, panel, u.at[z], sem_us.at[0, z], sem_u.at[z], dev(zz=lax.min(z + 1, nz - 1)))
    send(z > 0, panel, u.at[z], sem_us.at[1, z], sem_u.at[z], dev(zz=lax.max(z - 1, 0)))
    send(None, panel, own, sem_sib.at[0, y], sem_col.at[x, pr], sib)
    send(None, codes, crecv, sem_x.at[1], sem_x.at[2], xp)
    for g in range(groups):
        send(None, tiles.at[:, g, ox], srecv.at[:, g], sem_s.at[0, g], sem_s.at[1, g], xp)
    local = [pltpu.make_async_copy(panel, own, sem_l.at[0]),
             pltpu.make_async_copy(panel, u.at[z], sem_l.at[1])]
    for copy in local:
        copy.start()

    far = col.at[ox, pr]
    arrive(far, sem_col.at[ox, pr])
    for k, yy in enumerate(other_y):
        send(None, far, far, sem_y.at[1, k], sem_col.at[ox, pr], dev(yy=yy))
    send(None, far, far, sem_sib.at[1, y], sem_col.at[ox, pr], sib)
    for yy in other_y:
        p = yy * PAIR + c
        arrive(col.at[x, p], sem_col.at[x, p])
        send(None, col.at[x, p], col.at[x, p], sem_sib.at[0, yy], sem_col.at[x, p], sib)

    def relay(d):
        low, high = lax.max(z - d, 0), lax.min(z + d, nz - 1)

        @pl.when(z - d >= 0)
        def _():
            arrive(u.at[low], sem_u.at[low])
        send((z - d >= 0) & (z + 1 < nz), u.at[low], u.at[low], sem_us.at[0, low], sem_u.at[low],
             dev(zz=lax.min(z + 1, nz - 1)))

        @pl.when(z + d < nz)
        def _():
            arrive(u.at[high], sem_u.at[high])
        send((z + d < nz) & (z > 0), u.at[high], u.at[high], sem_us.at[1, high], sem_u.at[high],
             dev(zz=lax.max(z - 1, 0)))

    relay(1)
    for yy in other_y:
        p = yy * PAIR + c
        arrive(col.at[ox, p], sem_col.at[ox, p])
        send(None, col.at[ox, p], col.at[ox, p], sem_sib.at[1, yy], sem_col.at[ox, p], sib)
    for d in range(2, nz):
        relay(d)
    for xx in (x, ox):
        for yy in range(ny):
            p = yy * PAIR + oc
            arrive(col.at[xx, p], sem_col.at[xx, p])
    for copy in local:
        copy.wait()

    for h, xx in enumerate((x, ox)):
        @pl.loop(0, rows)
        def _(p):
            at = pl.multiple_of(p * share, share)
            for n in range(width // chunk):
                hi, lo = split(col[xx, p, :, n * chunk:(n + 1) * chunk])
                b_hi[n, h, pl.ds(at, share), :] = hi
                b_lo[n, h, pl.ds(at, share), :] = lo
    strip = 128
    for k in range(width // strip):
        piece = u[:, :, k * strip:(k + 1) * strip].reshape(nz * share, strip)
        hi, lo = split(piece.T)
        ut_hi[k * strip:(k + 1) * strip, :] = hi
        ut_lo[k * strip:(k + 1) * strip, :] = lo

    def place(h, source, marks):
        for zz in range(nz):
            level, g = zz * PAIR // per_tile, zz * PAIR % per_tile // PAIR
            total = jnp.zeros((share, block), F32)
            for k in range(slots):
                total += jnp.where(marks[k, 0:1, :] == level, source(k, g), 0.0)
            hi, lo = split(total)
            a_hi[h, zz * share:(zz + 1) * share, :] = hi
            a_lo[h, zz * share:(zz + 1) * share, :] = lo

    place(0, lambda k, g: tiles[k, g, x], codes)
    arrive(crecv, sem_x.at[2])
    for g in range(groups):
        arrive(srecv.at[:, g], sem_s.at[1, g])
    place(1, lambda k, g: srecv[k, g], crecv)

    up, down = dev(zz=lax.min(z + 1, nz - 1)), dev(zz=lax.max(z - 1, 0))

    def up_args(n, t):
        return (part.at[n, t], uprecv.at[n, t], sem_rss.at[n, t], sem_rs.at[0, n, t], up)

    def down_args(n, t):
        return (part.at[n, t], dnrecv.at[n, t], sem_rss.at[n, t], sem_rs.at[1, n, t], down)

    def sib_args(j):
        at = pl.ds(j * zj, zj)
        return (piv.at[oc, at], prec.at[at], sem_p.at[0, j], sem_p.at[1, j], sib)

    @pl.loop(0, supers)
    def _(j):
        for half in range(PAIR):
            n = j * PAIR + half
            product = (dot3(a_hi[0], a_lo[0], b_hi[n, 0], b_lo[n, 0])
                       + dot3(a_hi[1], a_lo[1], b_hi[n, 1], b_lo[n, 1]))
            part[n] = product.reshape(nz, share, chunk)
            for t in range(1, nz):
                @pl.when(z == 0)
                def _():
                    remote(*up_args(n, nz - t)).start()

                @pl.when(z == nz - 1)
                def _():
                    remote(*down_args(n, t - 1)).start()
            hi, lo = split(product)
            at = pl.ds(pl.multiple_of(j * block, block), block)
            update = dot3(ut_hi[at, :], ut_lo[at, :], hi, lo)
            piv[half, pl.ds(j * zj, zj)] = update.reshape(zj, PAIR, base.shape[0], chunk)
        remote(*sib_args(j)).start()

    for j in range(supers):
        pending.append((None, sib_args(j)))
    for n in range(width // chunk):
        for t in range(nz):
            pending.append((z < t, up_args(n, t)))
            pending.append((z > t, down_args(n, t)))

    def pass_on(n):
        for k in range(1, nz):
            t, b = nz - k, k - 1

            @pl.when((z > 0) & (z < t))
            def _():
                arrive(uprecv.at[n, t], sem_rs.at[0, n, t])
                part[n, t] = part[n, t] + uprecv[n, t]
                remote(*up_args(n, t)).start()

            @pl.when((z < nz - 1) & (z > b))
            def _():
                arrive(dnrecv.at[n, b], sem_rs.at[1, n, b])
                part[n, b] = part[n, b] + dnrecv[n, b]
                remote(*down_args(n, b)).start()

    def pivot_pair():
        for j in range(supers):
            at = pl.ds(j * zj, zj)
            arrive(prec.at[at], sem_p.at[1, j])
            piv[c, at] = piv[c, at] + prec[at]
            send(None, piv.at[c, at, ox], xrec.at[at], sem_px.at[0, j], sem_px.at[1, j], xp)

    def pivot_x():
        for j in range(supers):
            at = pl.ds(j * zj, zj)
            arrive(xrec.at[at], sem_px.at[1, j])
            piv[c, at, x] = piv[c, at, x] + xrec[at]
        for k, yy in enumerate(other_y):
            send(None, piv.at[c, pl.ds(yy * zset, zset), x], yrec.at[y], sem_pys.at[k], sem_py.at[y],
                 dev(yy=yy))

    mine = lax.div(z, zset) == y

    def pivot_y():
        at = pl.ds(y * zset, zset)
        for yy in other_y:
            arrive(yrec.at[yy], sem_py.at[yy])
            piv[c, at, x] = piv[c, at, x] + yrec[yy]
        for k in range(zset):
            t = y * zset + k
            send(t != z, piv.at[c, t, x], zrec.at[z], sem_pzs.at[k], sem_pz.at[z],
                 dev(zz=jnp.where(t != z, t, lax.rem(z + 1, nz))))

    def pivot_z():
        @pl.when(mine)
        def _():
            total = piv[c, z, x]
            for zz in other_z:
                arrive(zrec.at[zz], sem_pz.at[zz])
                total = total + zrec[zz]
            fin[c] = total
        send(mine, fin.at[c], fin.at[c], sem_fs.at[0], sem_f.at[c], sib)
        for k, yy in enumerate(other_y):
            for m, cc in enumerate((c, oc)):
                send(mine, fin.at[c], fin.at[c], sem_fs.at[1 + k * PAIR + m], sem_f.at[c],
                     dev(yy=yy, cc=cc))

    stages = [pivot_pair, pivot_x, pivot_y]
    for n in range(width // chunk):
        pass_on(n)
        if stages:
            stages.pop(0)()
    pivot_z()

    for n in range(width // chunk):
        at = slice(n * chunk, (n + 1) * chunk)
        out_panel[:, at] = -part[n, z]

        @pl.when(z > 0)
        def _():
            arrive(uprecv.at[n, z], sem_rs.at[0, n, z])
            out_panel[:, at] = out_panel[:, at] - uprecv[n, z]

        @pl.when(z < nz - 1)
        def _():
            arrive(dnrecv.at[n, z], sem_rs.at[1, n, z])
            out_panel[:, at] = out_panel[:, at] - dnrecv[n, z]

    @pl.when(jnp.logical_not(mine))
    def _():
        arrive(fin.at[c], sem_f.at[c])
    arrive(fin.at[oc], sem_f.at[oc])
    for half in range(PAIR):
        at = slice(half * chunk, (half + 1) * chunk)
        out_pivot[:, at] = base[:, at] + fin[half]

    for cond, args in pending:
        if cond is None:
            remote(*args).wait_send()
        else:
            @pl.when(cond)
            def _():
                remote(*args).wait_send()


def local(rows, cols, inverse_tiles, tile_rows, panel, pivot_base):
    slots, block, _ = inverse_tiles.shape
    share, width = panel.shape
    own_rows = pivot_base.shape[0]
    ny, nz = rows // PAIR, cols // PAIR
    chunk = block // PAIR
    chunks = width // chunk
    supers = width // block
    groups = block // share // PAIR
    zset = nz // ny
    tiles = inverse_tiles.reshape(slots, groups, PAIR, share, block)
    codes = jnp.broadcast_to(tile_rows[:, :, None], (slots, 8, block))
    dma, vmem = pltpu.SemaphoreType.DMA, pltpu.VMEM
    deep, tall = PAIR * block, nz * share
    return pl.pallas_call(
        functools.partial(kernel, rows, cols),
        out_shape=(jax.ShapeDtypeStruct((share, width), F32),
                   jax.ShapeDtypeStruct((own_rows, block), F32)),
        in_specs=[pl.BlockSpec(memory_space=pltpu.VMEM)] * 4,
        out_specs=[pl.BlockSpec(memory_space=pltpu.VMEM)] * 2,
        scratch_shapes=[
            vmem((PAIR, rows, share, width), F32),
            vmem((slots, groups, share, block), F32),
            vmem((slots, 8, block), jnp.int32),
            vmem((nz, share, width), F32),
            vmem((width, tall), BF16), vmem((width, tall), BF16),
            vmem((PAIR, tall, block), BF16), vmem((PAIR, tall, block), BF16),
            vmem((chunks, PAIR, block, chunk), BF16), vmem((chunks, PAIR, block, chunk), BF16),
            vmem((chunks, nz, share, chunk), F32),
            vmem((chunks, nz, share, chunk), F32),
            vmem((chunks, nz, share, chunk), F32),
            vmem((PAIR, nz, PAIR, own_rows, chunk), F32),
            vmem((nz, PAIR, own_rows, chunk), F32),
            vmem((nz, own_rows, chunk), F32),
            vmem((ny, zset, own_rows, chunk), F32),
            vmem((nz, own_rows, chunk), F32),
            vmem((PAIR, own_rows, chunk), F32),
            dma((PAIR, rows)), dma((PAIR, ny)), dma((3,)), dma((PAIR, ny)), dma((2, groups)),
            dma((nz,)), dma((2, nz)), dma((2, chunks, nz)), dma((chunks, nz)),
            dma((2, supers)), dma((2, supers)), dma((ny,)), dma((ny,)), dma((nz,)), dma((zset,)),
            dma((PAIR,)), dma((rows,)), dma((2,)),
        ],
        compiler_params=pltpu.CompilerParams(collective_id=0, has_side_effects=True),
    )(tiles, codes, panel, pivot_base)


def solution(mesh):
    return jax.shard_map(
        functools.partial(local, mesh.shape["prow"], mesh.shape["pcol"]),
        mesh=mesh,
        in_specs=(
            P("prow", "pcol", None),
            P("prow", "pcol"),
            P(("prow", "pcol"), None),
            P("pcol", None),
        ),
        out_specs=(P(("prow", "pcol"), None), P("pcol", None)),
        check_vma=False,
    )
```

```python
import functools

import jax
import jax.numpy as jnp
from jax import lax
from jax.experimental import pallas as pl
from jax.experimental.pallas import tpu as pltpu
from jax.sharding import PartitionSpec as P

F32 = jnp.float32
BF16 = jnp.bfloat16
PAIR = 2


def split(value):
    high = value.astype(BF16)
    return high, (value - high.astype(F32)).astype(BF16)


def dot3(a_hi, a_lo, b_hi, b_lo):
    dot = functools.partial(jnp.dot, preferred_element_type=F32)
    return dot(a_hi, b_hi) + (dot(a_hi, b_lo) + dot(a_lo, b_hi))


def kernel(rows, cols, tiles, codes, panel, base, out_panel, out_pivot,
           col, srecv, crecv, u, ut_hi, ut_lo, a_hi, a_lo, b_hi, b_lo, c_hi, c_lo, part, uprecv, dnrecv,
           piv, prec, xrec, yrec, zrec, fin,
           sem_col, sem_sib, sem_x, sem_y, sem_s, sem_u, sem_us, sem_rs, sem_rss,
           sem_p, sem_px, sem_py, sem_pys, sem_pz, sem_pzs, sem_f, sem_fs, sem_l):
    ny, nz = rows // PAIR, cols // PAIR
    slots, groups, _, share, block = tiles.shape
    width = panel.shape[1]
    chunk = block // PAIR
    supers = width // block
    per_tile = groups * PAIR
    zset = nz // ny
    zj = nz // supers
    pr, pc = lax.axis_index("prow"), lax.axis_index("pcol")
    c, y = lax.rem(pr, PAIR), lax.div(pr, PAIR)
    x, z = lax.rem(pc, PAIR), lax.div(pc, PAIR)
    oc, ox = 1 - c, 1 - x

    def dev(yy=None, cc=None, zz=None, xx=None):
        yy = y if yy is None else yy
        cc = c if cc is None else cc
        zz = z if zz is None else zz
        xx = x if xx is None else xx
        return (yy * PAIR + cc, zz * PAIR + xx)

    sib, xp = dev(cc=oc), dev(xx=ox)
    pending = []

    def remote(src, dst, send, recv, device):
        return pltpu.make_async_remote_copy(
            src_ref=src, dst_ref=dst, send_sem=send, recv_sem=recv,
            device_id=device, device_id_type=pl.DeviceIdType.MESH)

    def send(cond, *args):
        pending.append((cond, args))
        if cond is None:
            remote(*args).start()
        else:
            @pl.when(cond)
            def _():
                remote(*args).start()

    def arrive(dst, recv):
        remote(dst, dst, recv, recv, xp).wait_recv()

    other_y = [lax.rem(y + k, ny) for k in range(1, ny)]
    other_z = [lax.rem(z + k, nz) for k in range(1, nz)]

    barrier = pltpu.get_barrier_semaphore()
    peers = [dev(cc=oc), xp]
    for yy in other_y:
        peers += [dev(yy=yy), dev(yy=yy, cc=oc)]
    peers += [dev(zz=zz) for zz in other_z]
    for peer in peers:
        pl.semaphore_signal(barrier, inc=1, device_id=peer, device_id_type=pl.DeviceIdType.MESH)
    pl.semaphore_wait(barrier, len(peers))

    own = col.at[x, pr]
    send(None, panel, own, sem_x.at[0], sem_col.at[x, pr], xp)
    for k, yy in enumerate(other_y):
        send(None, panel, own, sem_y.at[0, k], sem_col.at[x, pr], dev(yy=yy))
    send(z + 1 < nz, panel, u.at[z], sem_us.at[0, z], sem_u.at[z], dev(zz=lax.min(z + 1, nz - 1)))
    send(z > 0, panel, u.at[z], sem_us.at[1, z], sem_u.at[z], dev(zz=lax.max(z - 1, 0)))
    send(None, panel, own, sem_sib.at[0, y], sem_col.at[x, pr], sib)
    send(None, codes, crecv, sem_x.at[1], sem_x.at[2], xp)
    for g in range(groups):
        send(None, tiles.at[:, g, ox], srecv.at[:, g], sem_s.at[0, g], sem_s.at[1, g], xp)
    local = [pltpu.make_async_copy(panel, own, sem_l.at[0]),
             pltpu.make_async_copy(panel, u.at[z], sem_l.at[1])]
    for copy in local:
        copy.start()

    far = col.at[ox, pr]
    arrive(far, sem_col.at[ox, pr])
    for k, yy in enumerate(other_y):
        send(None, far, far, sem_y.at[1, k], sem_col.at[ox, pr], dev(yy=yy))
    send(None, far, far, sem_sib.at[1, y], sem_col.at[ox, pr], sib)
    for yy in other_y:
        p = yy * PAIR + c
        arrive(col.at[x, p], sem_col.at[x, p])
        send(None, col.at[x, p], col.at[x, p], sem_sib.at[0, yy], sem_col.at[x, p], sib)

    def relay(d):
        low, high = lax.max(z - d, 0), lax.min(z + d, nz - 1)

        @pl.when(z - d >= 0)
        def _():
            arrive(u.at[low], sem_u.at[low])
        send((z - d >= 0) & (z + 1 < nz), u.at[low], u.at[low], sem_us.at[0, low], sem_u.at[low],
             dev(zz=lax.min(z + 1, nz - 1)))

        @pl.when(z + d < nz)
        def _():
            arrive(u.at[high], sem_u.at[high])
        send((z + d < nz) & (z > 0), u.at[high], u.at[high], sem_us.at[1, high], sem_u.at[high],
             dev(zz=lax.max(z - 1, 0)))

    relay(1)
    for yy in other_y:
        p = yy * PAIR + c
        arrive(col.at[ox, p], sem_col.at[ox, p])
        send(None, col.at[ox, p], col.at[ox, p], sem_sib.at[1, yy], sem_col.at[ox, p], sib)
    for d in range(2, nz - 1):
        relay(d)
    for xx in (x, ox):
        for yy in range(ny):
            p = yy * PAIR + oc
            arrive(col.at[xx, p], sem_col.at[xx, p])
    local[0].wait()

    for h, xx in enumerate((x, ox)):
        @pl.loop(0, rows)
        def _(p):
            at = pl.multiple_of(p * share, share)
            for n in range(width // chunk):
                hi, lo = split(col[xx, p, :, n * chunk:(n + 1) * chunk])
                b_hi[n, h, pl.ds(at, share), :] = hi
                b_lo[n, h, pl.ds(at, share), :] = lo

    levels = nz // groups

    def place(h, g, source, marks):
        for level in range(levels):
            total = jnp.zeros((share, block), F32)
            for k in range(slots):
                total += jnp.where(marks[k, 0:1, :] == level, source(k, g), 0.0)
            hi, lo = split(total)
            a_hi[g, h, level * share:(level + 1) * share, :] = hi
            a_lo[g, h, level * share:(level + 1) * share, :] = lo

    for g in range(groups):
        place(0, g, lambda k, g: tiles[k, g, x], codes)

    up, down = dev(zz=lax.min(z + 1, nz - 1)), dev(zz=lax.max(z - 1, 0))

    def up_args(n, t):
        return (part.at[n, t], uprecv.at[n, t], sem_rss.at[n, t], sem_rs.at[0, n, t], up)

    def down_args(n, t):
        return (part.at[n, t], dnrecv.at[n, t], sem_rss.at[n, t], sem_rs.at[1, n, t], down)

    def sib_args(j):
        at = pl.ds(j * zj, zj)
        return (piv.at[oc, at], prec.at[at], sem_p.at[0, j], sem_p.at[1, j], sib)

    def multiply(g):
        @pl.loop(0, supers)
        def _(j):
            for half in range(PAIR):
                n = j * PAIR + half
                product = (dot3(a_hi[g, 0], a_lo[g, 0], b_hi[n, 0], b_lo[n, 0])
                           + dot3(a_hi[g, 1], a_lo[g, 1], b_hi[n, 1], b_lo[n, 1]))
                hi, lo = split(product)
                for level in range(levels):
                    at = slice(level * share, (level + 1) * share)
                    t = level * groups + g
                    part[n, t] = product[at]
                    c_hi[n, t * share:(t + 1) * share, :] = hi[at]
                    c_lo[n, t * share:(t + 1) * share, :] = lo[at]
                for level in range(levels):
                    t, b = (levels - 1 - level) * groups + g, level * groups + g
                    if t > 1:
                        @pl.when(z == 0)
                        def _():
                            remote(*up_args(n, t)).start()
                    if b < nz - 2:
                        @pl.when(z == nz - 1)
                        def _():
                            remote(*down_args(n, b)).start()

    def update(n):
        j, half = n // PAIR, n % PAIR
        at = slice(j * block, (j + 1) * block)
        value = dot3(ut_hi[at, :], ut_lo[at, :], c_hi[n], c_lo[n])
        piv[half, j * zj:(j + 1) * zj] = value.reshape(zj, PAIR, base.shape[0], chunk)
        if half == PAIR - 1:
            send(None, *sib_args(j))

    for n in range(width // chunk):
        for t in range(nz):
            pending.append((z < t, up_args(n, t)))
            pending.append((z > t, down_args(n, t)))

    def pass_on(n, g):
        for level in range(levels):
            t, b = (levels - 1 - level) * groups + g, level * groups + g

            @pl.when((z > 0) & (z < t))
            def _():
                arrive(uprecv.at[n, t], sem_rs.at[0, n, t])
                part[n, t] = part[n, t] + uprecv[n, t]
                remote(*up_args(n, t)).start()

            @pl.when((z < nz - 1) & (z > b))
            def _():
                arrive(dnrecv.at[n, b], sem_rs.at[1, n, b])
                part[n, b] = part[n, b] + dnrecv[n, b]
                remote(*down_args(n, b)).start()

    def pivot_pair():
        for j in range(supers):
            at = pl.ds(j * zj, zj)
            arrive(prec.at[at], sem_p.at[1, j])
            piv[c, at] = piv[c, at] + prec[at]
            send(None, piv.at[c, at, ox], xrec.at[at], sem_px.at[0, j], sem_px.at[1, j], xp)

    def pivot_x():
        for j in range(supers):
            at = pl.ds(j * zj, zj)
            arrive(xrec.at[at], sem_px.at[1, j])
            piv[c, at, x] = piv[c, at, x] + xrec[at]
        for k, yy in enumerate(other_y):
            send(None, piv.at[c, pl.ds(yy * zset, zset), x], yrec.at[y], sem_pys.at[k], sem_py.at[y],
                 dev(yy=yy))

    mine = lax.div(z, zset) == y

    def pivot_y():
        at = pl.ds(y * zset, zset)
        for yy in other_y:
            arrive(yrec.at[yy], sem_py.at[yy])
            piv[c, at, x] = piv[c, at, x] + yrec[yy]
        for k in range(zset):
            t = y * zset + k
            send(t != z, piv.at[c, t, x], zrec.at[z], sem_pzs.at[k], sem_pz.at[z],
                 dev(zz=jnp.where(t != z, t, lax.rem(z + 1, nz))))

    def pivot_z():
        @pl.when(mine)
        def _():
            total = piv[c, z, x]
            for zz in other_z:
                arrive(zrec.at[zz], sem_pz.at[zz])
                total = total + zrec[zz]
            fin[c] = total
        send(mine, fin.at[c], fin.at[c], sem_fs.at[0], sem_f.at[c], sib)
        for k, yy in enumerate(other_y):
            for m, cc in enumerate((c, oc)):
                send(mine, fin.at[c], fin.at[c], sem_fs.at[1 + k * PAIR + m], sem_f.at[c],
                     dev(yy=yy, cc=cc))

    chunks = width // chunk
    done = [0] * groups
    for g in range(groups):
        if g > 0:
            for n in range(chunks // 2):
                pass_on(n, g - 1)
            done[g - 1] = chunks // 2
        else:
            arrive(crecv, sem_x.at[2])
        arrive(srecv.at[:, g], sem_s.at[1, g])
        place(1, g, lambda k, g: srecv[k, g], crecv)
        multiply(g)
    for n in range(chunks):
        @pl.when(z == 0)
        def _():
            remote(*up_args(n, 1)).start()

        @pl.when(z == nz - 1)
        def _():
            remote(*down_args(n, nz - 2)).start()
    relay(nz - 1)
    local[1].wait()
    strip = 128
    for k in range(width // strip):
        piece = u[:, :, k * strip:(k + 1) * strip].reshape(nz * share, strip)
        hi, lo = split(piece.T)
        ut_hi[k * strip:(k + 1) * strip, :] = hi
        ut_lo[k * strip:(k + 1) * strip, :] = lo
    for n in range(chunks):
        for g in range(groups - 1):
            if n >= done[g]:
                pass_on(n, g)
        update(n)
    stages = [pivot_pair, pivot_x, pivot_y]
    for n in range(chunks):
        pass_on(n, groups - 1)
        if stages:
            stages.pop(0)()
    pivot_z()

    for n in range(width // chunk):
        at = slice(n * chunk, (n + 1) * chunk)
        out_panel[:, at] = -part[n, z]

        @pl.when(z > 0)
        def _():
            arrive(uprecv.at[n, z], sem_rs.at[0, n, z])
            out_panel[:, at] = out_panel[:, at] - uprecv[n, z]

        @pl.when(z < nz - 1)
        def _():
            arrive(dnrecv.at[n, z], sem_rs.at[1, n, z])
            out_panel[:, at] = out_panel[:, at] - dnrecv[n, z]

    @pl.when(jnp.logical_not(mine))
    def _():
        arrive(fin.at[c], sem_f.at[c])
    arrive(fin.at[oc], sem_f.at[oc])
    for half in range(PAIR):
        at = slice(half * chunk, (half + 1) * chunk)
        out_pivot[:, at] = base[:, at] + fin[half]

    for cond, args in pending:
        if cond is None:
            remote(*args).wait_send()
        else:
            @pl.when(cond)
            def _():
                remote(*args).wait_send()


def local(rows, cols, inverse_tiles, tile_rows, panel, pivot_base):
    slots, block, _ = inverse_tiles.shape
    share, width = panel.shape
    own_rows = pivot_base.shape[0]
    ny, nz = rows // PAIR, cols // PAIR
    chunk = block // PAIR
    chunks = width // chunk
    supers = width // block
    groups = block // share // PAIR
    zset = nz // ny
    tiles = inverse_tiles.reshape(slots, groups, PAIR, share, block)
    codes = jnp.broadcast_to(tile_rows[:, :, None], (slots, 8, block))
    dma, vmem = pltpu.SemaphoreType.DMA, pltpu.VMEM
    deep, tall = PAIR * block, nz * share
    return pl.pallas_call(
        functools.partial(kernel, rows, cols),
        out_shape=(jax.ShapeDtypeStruct((share, width), F32),
                   jax.ShapeDtypeStruct((own_rows, block), F32)),
        in_specs=[pl.BlockSpec(memory_space=pltpu.VMEM)] * 4,
        out_specs=[pl.BlockSpec(memory_space=pltpu.VMEM)] * 2,
        scratch_shapes=[
            vmem((PAIR, rows, share, width), F32),
            vmem((slots, groups, share, block), F32),
            vmem((slots, 8, block), jnp.int32),
            vmem((nz, share, width), F32),
            vmem((width, tall), BF16), vmem((width, tall), BF16),
            vmem((groups, PAIR, tall // groups, block), BF16),
            vmem((groups, PAIR, tall // groups, block), BF16),
            vmem((chunks, PAIR, block, chunk), BF16), vmem((chunks, PAIR, block, chunk), BF16),
            vmem((chunks, tall, chunk), BF16), vmem((chunks, tall, chunk), BF16),
            vmem((chunks, nz, share, chunk), F32),
            vmem((chunks, nz, share, chunk), F32),
            vmem((chunks, nz, share, chunk), F32),
            vmem((PAIR, nz, PAIR, own_rows, chunk), F32),
            vmem((nz, PAIR, own_rows, chunk), F32),
            vmem((nz, own_rows, chunk), F32),
            vmem((ny, zset, own_rows, chunk), F32),
            vmem((nz, own_rows, chunk), F32),
            vmem((PAIR, own_rows, chunk), F32),
            dma((PAIR, rows)), dma((PAIR, ny)), dma((3,)), dma((PAIR, ny)), dma((2, groups)),
            dma((nz,)), dma((2, nz)), dma((2, chunks, nz)), dma((chunks, nz)),
            dma((2, supers)), dma((2, supers)), dma((ny,)), dma((ny,)), dma((nz,)), dma((zset,)),
            dma((PAIR,)), dma((rows,)), dma((2,)),
        ],
        compiler_params=pltpu.CompilerParams(collective_id=0, has_side_effects=True),
    )(tiles, codes, panel, pivot_base)


def solution(mesh):
    return jax.shard_map(
        functools.partial(local, mesh.shape["prow"], mesh.shape["pcol"]),
        mesh=mesh,
        in_specs=(
            P("prow", "pcol", None),
            P("prow", "pcol"),
            P(("prow", "pcol"), None),
            P("pcol", None),
        ),
        out_specs=(P(("prow", "pcol"), None), P("pcol", None)),
        check_vma=False,
    )
```

```python
import functools

import jax
import jax.numpy as jnp
from jax import lax
from jax.experimental import pallas as pl
from jax.experimental.pallas import tpu as pltpu
from jax.sharding import PartitionSpec as P

F32 = jnp.float32
BF16 = jnp.bfloat16
PAIR = 2


def split(value):
    high = value.astype(BF16)
    return high, (value - high.astype(F32)).astype(BF16)


def dot3(a_hi, a_lo, b_hi, b_lo):
    dot = functools.partial(jnp.dot, preferred_element_type=F32)
    return dot(a_hi, b_hi) + (dot(a_hi, b_lo) + dot(a_lo, b_hi))


def kernel(rows, cols, tiles, codes, panel, base, out_panel, out_pivot,
           col, srecv, crecv, u, ut_hi, ut_lo, a_hi, a_lo, b_hi, b_lo, c_hi, c_lo, part, uprecv, dnrecv,
           piv, prec, xrec, yrec, zrec, fin,
           sem_col, sem_sib, sem_x, sem_y, sem_s, sem_u, sem_us, sem_rs, sem_rss,
           sem_p, sem_px, sem_py, sem_pys, sem_pz, sem_pzs, sem_f, sem_fs, sem_l):
    ny, nz = rows // PAIR, cols // PAIR
    slots, groups, _, share, block = tiles.shape
    width = panel.shape[1]
    chunk = block // PAIR
    supers = width // block
    per_tile = groups * PAIR
    zset = nz // ny
    zj = nz // supers
    pr, pc = lax.axis_index("prow"), lax.axis_index("pcol")
    c, y = lax.rem(pr, PAIR), lax.div(pr, PAIR)
    x, z = lax.rem(pc, PAIR), lax.div(pc, PAIR)
    oc, ox = 1 - c, 1 - x

    def dev(yy=None, cc=None, zz=None, xx=None):
        yy = y if yy is None else yy
        cc = c if cc is None else cc
        zz = z if zz is None else zz
        xx = x if xx is None else xx
        return (yy * PAIR + cc, zz * PAIR + xx)

    sib, xp = dev(cc=oc), dev(xx=ox)
    pending = []

    def remote(src, dst, send, recv, device):
        return pltpu.make_async_remote_copy(
            src_ref=src, dst_ref=dst, send_sem=send, recv_sem=recv,
            device_id=device, device_id_type=pl.DeviceIdType.MESH)

    def send(cond, *args):
        pending.append((cond, args))
        if cond is None:
            remote(*args).start()
        else:
            @pl.when(cond)
            def _():
                remote(*args).start()

    def arrive(dst, recv):
        remote(dst, dst, recv, recv, xp).wait_recv()

    other_y = [lax.rem(y + k, ny) for k in range(1, ny)]
    other_z = [lax.rem(z + k, nz) for k in range(1, nz)]

    barrier = pltpu.get_barrier_semaphore()
    peers = [dev(cc=oc), xp]
    for yy in other_y:
        peers += [dev(yy=yy), dev(yy=yy, cc=oc)]
    peers += [dev(zz=zz) for zz in other_z]
    for peer in peers:
        pl.semaphore_signal(barrier, inc=1, device_id=peer, device_id_type=pl.DeviceIdType.MESH)
    pl.semaphore_wait(barrier, len(peers))

    own = col.at[x, pr]
    send(None, panel, own, sem_x.at[0], sem_col.at[x, pr], xp)
    for k, yy in enumerate(other_y):
        send(None, panel, own, sem_y.at[0, k], sem_col.at[x, pr], dev(yy=yy))
    send(z + 1 < nz, panel, u.at[z], sem_us.at[0, z], sem_u.at[z], dev(zz=lax.min(z + 1, nz - 1)))
    send(z > 0, panel, u.at[z], sem_us.at[1, z], sem_u.at[z], dev(zz=lax.max(z - 1, 0)))
    send(None, panel, own, sem_sib.at[0, y], sem_col.at[x, pr], sib)
    send(None, codes, crecv, sem_x.at[1], sem_x.at[2], xp)
    for g in range(groups):
        send(None, tiles.at[:, g, ox], srecv.at[:, g], sem_s.at[0, g], sem_s.at[1, g], xp)
    local = [pltpu.make_async_copy(panel, own, sem_l.at[0]),
             pltpu.make_async_copy(panel, u.at[z], sem_l.at[1])]
    for copy in local:
        copy.start()

    far = col.at[ox, pr]
    arrive(far, sem_col.at[ox, pr])
    for k, yy in enumerate(other_y):
        send(None, far, far, sem_y.at[1, k], sem_col.at[ox, pr], dev(yy=yy))
    send(None, far, far, sem_sib.at[1, y], sem_col.at[ox, pr], sib)
    for yy in other_y:
        p = yy * PAIR + c
        arrive(col.at[x, p], sem_col.at[x, p])
        send(None, col.at[x, p], col.at[x, p], sem_sib.at[0, yy], sem_col.at[x, p], sib)

    def relay(d):
        low, high = lax.max(z - d, 0), lax.min(z + d, nz - 1)

        @pl.when(z - d >= 0)
        def _():
            arrive(u.at[low], sem_u.at[low])
        send((z - d >= 0) & (z + 1 < nz), u.at[low], u.at[low], sem_us.at[0, low], sem_u.at[low],
             dev(zz=lax.min(z + 1, nz - 1)))

        @pl.when(z + d < nz)
        def _():
            arrive(u.at[high], sem_u.at[high])
        send((z + d < nz) & (z > 0), u.at[high], u.at[high], sem_us.at[1, high], sem_u.at[high],
             dev(zz=lax.max(z - 1, 0)))

    relay(1)
    for yy in other_y:
        p = yy * PAIR + c
        arrive(col.at[ox, p], sem_col.at[ox, p])
        send(None, col.at[ox, p], col.at[ox, p], sem_sib.at[1, yy], sem_col.at[ox, p], sib)
    for d in range(2, nz - 1):
        relay(d)
    for xx in (x, ox):
        for yy in range(ny):
            p = yy * PAIR + oc
            arrive(col.at[xx, p], sem_col.at[xx, p])
    local[0].wait()

    for h, xx in enumerate((x, ox)):
        @pl.loop(0, rows)
        def _(p):
            at = pl.multiple_of(p * share, share)
            for n in range(width // chunk):
                hi, lo = split(col[xx, p, :, n * chunk:(n + 1) * chunk])
                b_hi[n, h, pl.ds(at, share), :] = hi
                b_lo[n, h, pl.ds(at, share), :] = lo

    levels = nz // groups

    def place(h, g, source, marks):
        for level in range(levels):
            total = jnp.zeros((share, block), F32)
            for k in range(slots):
                total += jnp.where(marks[k, 0:1, :] == level, source(k, g), 0.0)
            hi, lo = split(total)
            a_hi[g, h, level * share:(level + 1) * share, :] = hi
            a_lo[g, h, level * share:(level + 1) * share, :] = lo

    for g in range(groups):
        place(0, g, lambda k, g: tiles[k, g, x], codes)

    up, down = dev(zz=lax.min(z + 1, nz - 1)), dev(zz=lax.max(z - 1, 0))

    def up_args(n, t):
        return (part.at[n, t], uprecv.at[n, t], sem_rss.at[n, t], sem_rs.at[0, n, t], up)

    def down_args(n, t):
        return (part.at[n, t], dnrecv.at[n, t], sem_rss.at[n, t], sem_rs.at[1, n, t], down)

    def sib_args(j):
        at = pl.ds(j * zj, zj)
        return (piv.at[oc, at], prec.at[at], sem_p.at[0, j], sem_p.at[1, j], sib)

    def multiply(g):
        @pl.loop(0, supers)
        def _(j):
            for half in range(PAIR):
                n = j * PAIR + half
                product = (dot3(a_hi[g, 0], a_lo[g, 0], b_hi[n, 0], b_lo[n, 0])
                           + dot3(a_hi[g, 1], a_lo[g, 1], b_hi[n, 1], b_lo[n, 1]))
                hi, lo = split(product)
                for level in range(levels):
                    at = slice(level * share, (level + 1) * share)
                    t = level * groups + g
                    part[n, t] = product[at]
                    c_hi[n, t * share:(t + 1) * share, :] = hi[at]
                    c_lo[n, t * share:(t + 1) * share, :] = lo[at]
                for level in range(levels):
                    t, b = (levels - 1 - level) * groups + g, level * groups + g
                    if t > 1:
                        @pl.when(z == 0)
                        def _():
                            remote(*up_args(n, t)).start()
                    if b < nz - 2:
                        @pl.when(z == nz - 1)
                        def _():
                            remote(*down_args(n, b)).start()

    def update(n):
        j, half = n // PAIR, n % PAIR
        at = slice(j * block, (j + 1) * block)
        value = dot3(ut_hi[at, :], ut_lo[at, :], c_hi[n], c_lo[n])
        piv[half, j * zj:(j + 1) * zj] = value.reshape(zj, PAIR, base.shape[0], chunk)
        if half == PAIR - 1:
            send(None, *sib_args(j))

    for n in range(width // chunk):
        for t in range(nz):
            pending.append((z < t, up_args(n, t)))
            pending.append((z > t, down_args(n, t)))

    def pass_on(n, g):
        for level in range(levels):
            t, b = (levels - 1 - level) * groups + g, level * groups + g

            @pl.when((z > 0) & (z < t))
            def _():
                arrive(uprecv.at[n, t], sem_rs.at[0, n, t])
                part[n, t] = part[n, t] + uprecv[n, t]
                remote(*up_args(n, t)).start()

            @pl.when((z < nz - 1) & (z > b))
            def _():
                arrive(dnrecv.at[n, b], sem_rs.at[1, n, b])
                part[n, b] = part[n, b] + dnrecv[n, b]
                remote(*down_args(n, b)).start()

    def x_first(j):
        return j % 2 == 0

    def y_args(j, k, m, to, sender):
        t = j * zj + k * ny + to
        if x_first(j):
            return (piv.at[c, t, x], yrec.at[sender, j, k, 0], sem_pys.at[m, j, k], sem_py.at[sender, j, k],
                    dev(yy=to))
        return (piv.at[c, t], yrec.at[sender, j, k], sem_pys.at[m, j, k], sem_py.at[sender, j, k],
                dev(yy=to))

    def send_y(j):
        for m, yy in enumerate(other_y):
            for k in range(zset // supers):
                send(None, *y_args(j, k, m, yy, y))

    def add_y(j):
        for yy in other_y:
            for k in range(zset // supers):
                t = j * zj + k * ny + y
                if x_first(j):
                    arrive(yrec.at[yy, j, k, 0], sem_py.at[yy, j, k])
                    piv[c, t, x] = piv[c, t, x] + yrec[yy, j, k, 0]
                else:
                    arrive(yrec.at[yy, j, k], sem_py.at[yy, j, k])
                    piv[c, t] = piv[c, t] + yrec[yy, j, k]

    def pivot_pair(j):
        at = pl.ds(j * zj, zj)
        arrive(prec.at[at], sem_p.at[1, j])
        piv[c, at] = piv[c, at] + prec[at]
        if x_first(j):
            send(None, piv.at[c, at, ox], xrec.at[at], sem_px.at[0, j * zj], sem_px.at[1, j * zj], xp)
        else:
            send_y(j)

    def pivot_one(j):
        at = pl.ds(j * zj, zj)
        if x_first(j):
            arrive(xrec.at[at], sem_px.at[1, j * zj])
            piv[c, at, x] = piv[c, at, x] + xrec[at]
            send_y(j)
        else:
            add_y(j)
            for k in range(zset // supers):
                t = j * zj + k * ny + y
                send(None, piv.at[c, t, ox], xrec.at[t], sem_px.at[0, t], sem_px.at[1, t], xp)

    def pivot_two(j):
        if x_first(j):
            add_y(j)
        else:
            for k in range(zset // supers):
                t = j * zj + k * ny + y
                arrive(xrec.at[t], sem_px.at[1, t])
                piv[c, t, x] = piv[c, t, x] + xrec[t]
        for k in range(zset // supers):
            t = j * zj + k * ny + y
            send(t != z, piv.at[c, t, x], zrec.at[z], sem_pzs.at[j, k], sem_pz.at[z],
                 dev(zz=jnp.where(t != z, t, lax.rem(z + 1, nz))))

    mine = lax.rem(z, ny) == y

    def pivot_z():
        @pl.when(mine)
        def _():
            total = piv[c, z, x]
            for zz in other_z:
                arrive(zrec.at[zz], sem_pz.at[zz])
                total = total + zrec[zz]
            fin[c] = total
        for k, yy in enumerate(other_y):
            send(mine, fin.at[c], fin.at[c], sem_fs.at[1 + k], sem_f.at[c], dev(yy=yy))

        @pl.when(jnp.logical_not(mine))
        def _():
            arrive(fin.at[c], sem_f.at[c])
        send(None, fin.at[c], fin.at[c], sem_fs.at[0], sem_f.at[c], sib)

    chunks = width // chunk
    done = [0] * groups
    for g in range(groups):
        if g > 0:
            for n in range(chunks // 2):
                pass_on(n, g - 1)
            done[g - 1] = chunks // 2
        else:
            arrive(crecv, sem_x.at[2])
        arrive(srecv.at[:, g], sem_s.at[1, g])
        place(1, g, lambda k, g: srecv[k, g], crecv)
        multiply(g)
    for n in range(chunks):
        @pl.when(z == 0)
        def _():
            remote(*up_args(n, 1)).start()

        @pl.when(z == nz - 1)
        def _():
            remote(*down_args(n, nz - 2)).start()
    relay(nz - 1)
    local[1].wait()
    strip = 128
    for k in range(width // strip):
        piece = u[:, :, k * strip:(k + 1) * strip].reshape(nz * share, strip)
        hi, lo = split(piece.T)
        ut_hi[k * strip:(k + 1) * strip, :] = hi
        ut_lo[k * strip:(k + 1) * strip, :] = lo
    for n in range(chunks):
        for g in range(groups - 1):
            if n >= done[g]:
                pass_on(n, g)
        update(n)
    for n in range(chunks):
        pass_on(n, groups - 1)
        if n < supers:
            pivot_pair(n)
        elif n == supers:
            for j in range(supers):
                pivot_one(j)
    for j in range(supers):
        pivot_two(j)

    for n in range(width // chunk):
        at = slice(n * chunk, (n + 1) * chunk)
        out_panel[:, at] = -part[n, z]

        @pl.when(z > 0)
        def _():
            arrive(uprecv.at[n, z], sem_rs.at[0, n, z])
            out_panel[:, at] = out_panel[:, at] - uprecv[n, z]

        @pl.when(z < nz - 1)
        def _():
            arrive(dnrecv.at[n, z], sem_rs.at[1, n, z])
            out_panel[:, at] = out_panel[:, at] - dnrecv[n, z]

    pivot_z()
    arrive(fin.at[oc], sem_f.at[oc])
    for half in range(PAIR):
        at = slice(half * chunk, (half + 1) * chunk)
        out_pivot[:, at] = base[:, at] + fin[half]

    for cond, args in pending:
        if cond is None:
            remote(*args).wait_send()
        else:
            @pl.when(cond)
            def _():
                remote(*args).wait_send()


def local(rows, cols, inverse_tiles, tile_rows, panel, pivot_base):
    slots, block, _ = inverse_tiles.shape
    share, width = panel.shape
    own_rows = pivot_base.shape[0]
    ny, nz = rows // PAIR, cols // PAIR
    chunk = block // PAIR
    chunks = width // chunk
    supers = width // block
    groups = block // share // PAIR
    zset = nz // ny
    tiles = inverse_tiles.reshape(slots, groups, PAIR, share, block)
    codes = jnp.broadcast_to(tile_rows[:, :, None], (slots, 8, block))
    dma, vmem = pltpu.SemaphoreType.DMA, pltpu.VMEM
    deep, tall = PAIR * block, nz * share
    return pl.pallas_call(
        functools.partial(kernel, rows, cols),
        out_shape=(jax.ShapeDtypeStruct((share, width), F32),
                   jax.ShapeDtypeStruct((own_rows, block), F32)),
        in_specs=[pl.BlockSpec(memory_space=pltpu.VMEM)] * 4,
        out_specs=[pl.BlockSpec(memory_space=pltpu.VMEM)] * 2,
        scratch_shapes=[
            vmem((PAIR, rows, share, width), F32),
            vmem((slots, groups, share, block), F32),
            vmem((slots, 8, block), jnp.int32),
            vmem((nz, share, width), F32),
            vmem((width, tall), BF16), vmem((width, tall), BF16),
            vmem((groups, PAIR, tall // groups, block), BF16),
            vmem((groups, PAIR, tall // groups, block), BF16),
            vmem((chunks, PAIR, block, chunk), BF16), vmem((chunks, PAIR, block, chunk), BF16),
            vmem((chunks, tall, chunk), BF16), vmem((chunks, tall, chunk), BF16),
            vmem((chunks, nz, share, chunk), F32),
            vmem((chunks, nz, share, chunk), F32),
            vmem((chunks, nz, share, chunk), F32),
            vmem((PAIR, nz, PAIR, own_rows, chunk), F32),
            vmem((nz, PAIR, own_rows, chunk), F32),
            vmem((nz, own_rows, chunk), F32),
            vmem((ny, supers, zset // supers, PAIR, own_rows, chunk), F32),
            vmem((nz, own_rows, chunk), F32),
            vmem((PAIR, own_rows, chunk), F32),
            dma((PAIR, rows)), dma((PAIR, ny)), dma((3,)), dma((PAIR, ny)), dma((2, groups)),
            dma((nz,)), dma((2, nz)), dma((2, chunks, nz)), dma((chunks, nz)),
            dma((2, supers)), dma((2, nz)), dma((ny, supers, zset // supers)), dma((ny, supers, zset // supers)),
            dma((nz,)), dma((supers, zset // supers)),
            dma((PAIR,)), dma((rows,)), dma((2,)),
        ],
        compiler_params=pltpu.CompilerParams(collective_id=0, has_side_effects=True),
    )(tiles, codes, panel, pivot_base)


def solution(mesh):
    return jax.shard_map(
        functools.partial(local, mesh.shape["prow"], mesh.shape["pcol"]),
        mesh=mesh,
        in_specs=(
            P("prow", "pcol", None),
            P("prow", "pcol"),
            P(("prow", "pcol"), None),
            P("pcol", None),
        ),
        out_specs=(P(("prow", "pcol"), None), P("pcol", None)),
        check_vma=False,
    )
```
